128 devices in a mesh: seq: 16 (over z, x), head: 8 (over y, core).
Axes of the slice: x: 4, y: 4, z: 4, core: 2. Of those that a mesh axis runs over, the one named last changes fastest.
Arguments:
- tokens: bfloat16 [16384, 4096], P('seq'), may hold values from -6 to 6
- w_query: bfloat16 [4096, 4096], P(None, 'head'), may hold values from -0.09375 to 0.09375
- w_key: bfloat16 [4096, 4096], P(None, 'head'), may hold values from -0.09375 to 0.09375
- w_value: bfloat16 [4096, 4096], P(None, 'head'), may hold values from -0.09375 to 0.09375
- norm_gain: float32 [4096], P('head'), may hold values from 0.25 to 1.75
- w_out: bfloat16 [4096, 4096], P('head'), may hold values from -0.125 to 0.125
Outputs:
- mixed: bfloat16 [16384, 4096], P('seq', 'head')
The draws below stay inside these ranges and needn't reach their ends.
All inputs are finite; a program needn't handle non-finite values.
Results may differ from the reference program's by a relative error of at most 0.02.
Values may be sent and summed in bfloat16 or wider, within the bound.
No kernel may reach another device: no remote copies, remote signals or barrier semaphores. Data moves between devices by JAX's collectives and lax.ppermute only.
A program may use at most 128 MiB of HBM per device.

```python
import jax
import jax.numpy as jnp
from jax import lax

D = 4096
HEADS = 32
HEAD_DIM = 128
SPAN = 128
TOKENS = 16384
N_HEAD = 8


def spiked(result, rng, source, target, shards_of, factor):
    owner, partner = [(jnp.arange(result.shape[position]) // (result.shape[position] // shards_of)).reshape([-1 if axis == position else 1 for axis in range(result.ndim)]) for position in (source, target)]
    chosen = jax.random.permutation(rng, shards_of)[partner]
    strong = (owner == chosen) | (owner == (partner + shards_of // 2) % shards_of)
    return jnp.where(strong, factor * result, result)


def level_of(key, extent, split, least, top_value):
    loudness = 1.0
    for axis_at, blocks in split:
        draws = jax.random.uniform(jax.random.fold_in(jax.random.fold_in(key, 6), axis_at), (blocks,), jnp.float32, least / len(split), top_value / len(split))
        loudness = loudness * jnp.repeat(jnp.exp(draws), extent[axis_at] // blocks).reshape((-1,) + (1,) * (len(extent) - 1 - axis_at))
    return loudness


def noise(key, shape, scale, limit, cuts=(), held_as=jnp.bfloat16):
    result = scale * jax.random.normal(key, shape, jnp.float32)
    if cuts:
        result = result * level_of(key, shape, cuts, -0.22, 0.18)
    return jnp.clip(result, -limit, limit).astype(held_as)


def bell_draw_with(rng, extent, scale, bound, cuts, heavy, kind=jnp.bfloat16):
    array = scale * jax.random.normal(rng, extent, jnp.float32)
    if cuts:
        array = array * level_of(rng, extent, cuts, -0.22, 0.18)
    return jnp.clip(spiked(array, jax.random.fold_in(rng, 3), *heavy), -bound, bound).astype(kind)


def setup_inputs(seed: int = 0) -> dict:
    keys = jax.random.split(jax.random.key(seed), 7)
    return {
        "tokens": noise(keys[0], (TOKENS, D), 1.0, 6.0, ((0, 16),)),
        "w_query": noise(keys[1], (D, D), D ** -0.5, 0.09375, ((1, 8),)),
        "w_key": noise(keys[2], (D, D), D ** -0.5, 0.09375, ((1, 8),)),
        "w_value": noise(keys[3], (D, D), D ** -0.5, 0.09375, ((1, 8),)),
        "norm_gain": jnp.clip(1.0 + 0.15 * jax.random.normal(keys[4], (D,), jnp.float32), 0.25, 1.75),
        "w_out": bell_draw_with(keys[5], (D, D), D ** -0.5, 0.125, ((0, 8),), (0, 1, 8, 2.0)),
    }


def lower_mask(size):
    rows = lax.broadcasted_iota(jnp.int32, (size, size), 0)
    cols = lax.broadcasted_iota(jnp.int32, (size, size), 1)
    return (rows >= cols).astype(jnp.float32)

def reference(tokens, w_query, w_key, w_value, norm_gain, w_out):
    count = tokens.shape[0]
    blocks = count // SPAN
    shape4 = (blocks, SPAN, HEADS, HEAD_DIM)
    q_rows = jnp.dot(tokens, w_query, preferred_element_type=jnp.float32).astype(jnp.bfloat16).reshape(shape4)
    k_rows = jnp.dot(tokens, w_key, preferred_element_type=jnp.float32).astype(jnp.bfloat16).reshape(shape4)
    v_rows = jnp.dot(tokens, w_value, preferred_element_type=jnp.float32).astype(jnp.bfloat16).reshape(shape4)
    masking = lower_mask(SPAN)

    def advance(state, pieces):
        q_blk, k_blk, v_blk = pieces
        q_f = q_blk.astype(jnp.float32)
        k_f = k_blk.astype(jnp.float32)
        v_f = v_blk.astype(jnp.float32)
        scores = (jnp.einsum('ihd,jhd->hij', q_f, k_f) * masking).astype(jnp.bfloat16)
        within = jnp.einsum('hij,jhe->ihe', scores.astype(jnp.float32), v_f)
        prior = state.astype(jnp.bfloat16).astype(jnp.float32)
        across = jnp.einsum('ihd,hde->ihe', q_f, prior)
        new_state = state + jnp.einsum('jhd,jhe->hde', k_f, v_f)
        return (new_state, within + across)
    start_state = jnp.zeros((HEADS, HEAD_DIM, HEAD_DIM), jnp.float32)
    final_state, raw = lax.scan(advance, start_state, (q_rows, k_rows, v_rows))
    power = lax.optimization_barrier(jnp.mean(raw * raw, axis=-1, keepdims=True))
    normed = raw * lax.rsqrt(power + 1e-06) * norm_gain.reshape(HEADS, HEAD_DIM)
    attended = normed.astype(jnp.bfloat16).reshape(count, D)
    group_width = D // N_HEAD
    grouped = attended.reshape(count, N_HEAD, group_width).transpose(1, 0, 2)
    out_rows = w_out.reshape(N_HEAD, group_width, D)

    def add_group(total, pieces):
        left, right = pieces
        partial_sum = jnp.dot(left, right, preferred_element_type=jnp.float32).astype(jnp.bfloat16)
        partial_sum = lax.optimization_barrier(partial_sum)
        return (total + partial_sum.astype(jnp.float32), None)
    summed, unused = lax.scan(add_group, jnp.zeros((count, D), jnp.float32), (grouped, out_rows))
    return summed.astype(jnp.bfloat16)
```

```python
import jax
import jax.numpy as jnp
from jax import lax
from jax.experimental import pallas as pl
from jax.experimental.pallas import tpu as pltpu
from jax.sharding import PartitionSpec as P

HEAD_DIM = 128
BLOCK = 256
F32, BF16 = jnp.float32, jnp.bfloat16
VMEM_LIMIT = 56 * 2**20


def dot(a, b):
    return jnp.dot(a, b, preferred_element_type=F32)


def dot_t(a, b, da, db):
    return lax.dot_general(a, b, (((da,), (db,)), ((), ())), preferred_element_type=F32)


def params(**kw):
    return pltpu.CompilerParams(vmem_limit_bytes=VMEM_LIMIT, **kw)


def cost(flops, nbytes):
    return pl.CostEstimate(flops=int(flops), bytes_accessed=int(nbytes), transcendentals=0)


CHUNKS = 8
TILE = 256


def project(tokens, weights, states):
    count, depth = tokens.shape
    width = weights[0].shape[1]
    n_w = len(weights)
    parts = width // TILE
    tiles = parts * n_w
    piece = depth // CHUNKS
    heads_tile = TILE // HEAD_DIM
    heads = width // HEAD_DIM

    def kernel(*refs):
        t_hbm, w_hbm = refs[0], refs[1 : 1 + n_w]
        outs = refs[1 + n_w : 1 + 2 * n_w]
        rest = refs[1 + 2 * n_w :]
        s_ref, rest = (rest[0], rest[1:]) if states else (None, rest)
        t_buf, w_buf, acc, t_sem, w0_sem, w_sem = rest

        def t_copy(k):
            cols = pl.ds(k * piece, piece)
            return pltpu.make_async_copy(t_hbm.at[:, cols], t_buf.at[:, cols], t_sem.at[k])

        def w0_copy(k):
            rows = pl.ds(k * piece, piece)
            return pltpu.make_async_copy(
                w_hbm[0].at[rows, pl.ds(0, TILE)], w_buf.at[0, rows, :], w0_sem.at[k]
            )

        def w_copy(n):
            part, which = n // n_w, n % n_w
            return pltpu.make_async_copy(
                w_hbm[which].at[:, pl.ds(part * TILE, TILE)], w_buf.at[n], w_sem.at[n]
            )

        for k in range(CHUNKS):
            t_copy(k).start()
            w0_copy(k).start()
        for n in range(1, tiles):
            w_copy(n).start()

        for k in range(CHUNKS):
            t_copy(k).wait()
            w0_copy(k).wait()
            cols = slice(k * piece, (k + 1) * piece)
            product = dot(t_buf[:, cols], w_buf[0, cols, :])
            if k == 0:
                acc[...] = product
            elif k < CHUNKS - 1:
                acc[...] += product
            else:
                outs[0][:, :TILE] = (acc[...] + product).astype(BF16)
        for n in range(1, tiles):
            part, which = n // n_w, n % n_w
            w_copy(n).wait()
            outs[which][:, part * TILE : (part + 1) * TILE] = dot(t_buf[...], w_buf[n]).astype(BF16)
            if states and which == n_w - 1:
                for j in range(heads_tile):
                    h = part * heads_tile + j
                    cols = slice(h * HEAD_DIM, (h + 1) * HEAD_DIM)
                    s_ref[cols, :] = dot_t(outs[0][:, cols], outs[1][:, cols], 0, 0).astype(BF16)

    out_shape = [jax.ShapeDtypeStruct((count, width), BF16)] * n_w
    if states:
        out_shape = out_shape + [jax.ShapeDtypeStruct((heads * HEAD_DIM, HEAD_DIM), BF16)]
    return pl.pallas_call(
        kernel,
        out_shape=out_shape,
        in_specs=[pl.BlockSpec(memory_space=pl.ANY)] * (1 + n_w),
        out_specs=[pl.BlockSpec(memory_space=pltpu.VMEM)] * len(out_shape),
        scratch_shapes=[
            pltpu.VMEM((count, depth), BF16),
            pltpu.VMEM((tiles, depth, TILE), BF16),
            pltpu.VMEM((count, TILE), F32),
            pltpu.SemaphoreType.DMA((CHUNKS,)),
            pltpu.SemaphoreType.DMA((CHUNKS,)),
            pltpu.SemaphoreType.DMA((tiles,)),
        ],
        compiler_params=params(),
        cost_estimate=cost(2 * count * depth * width * n_w, 2 * depth * (count + width * n_w)),
        name="project_kv" if states else "project_q",
    )(tokens, *weights)


def local_attention(q, k, v):
    count, width = q.shape
    heads = width // HEAD_DIM
    blocks = count // BLOCK

    def kernel(q_ref, k_ref, v_ref, w_ref, e_ref):
        rows = lax.broadcasted_iota(jnp.int32, (BLOCK, BLOCK), 0)
        cols = lax.broadcasted_iota(jnp.int32, (BLOCK, BLOCK), 1)
        keep = rows >= cols
        state = jnp.zeros((HEAD_DIM, HEAD_DIM), F32)
        for b in range(blocks):
            at = slice(b * BLOCK, (b + 1) * BLOCK)
            kb, vb = k_ref[at, :], v_ref[at, :]
            scores = jnp.where(keep, dot_t(q_ref[at, :], kb, 1, 1), 0.0).astype(BF16)
            w_ref[at, :] = dot(scores, vb)
            e_ref[b, 0] = state
            if b < blocks - 1:
                state = state + dot_t(kb, vb, 0, 0)

    spec = pl.BlockSpec((count, HEAD_DIM), lambda h: (0, h))
    return pl.pallas_call(
        kernel,
        grid=(heads,),
        out_shape=[
            jax.ShapeDtypeStruct((count, width), F32),
            jax.ShapeDtypeStruct((blocks, heads, HEAD_DIM, HEAD_DIM), F32),
        ],
        in_specs=[spec] * 3,
        out_specs=[spec, pl.BlockSpec((blocks, 1, HEAD_DIM, HEAD_DIM), lambda h: (0, h, 0, 0))],
        compiler_params=params(),
        cost_estimate=cost(4 * count * width * (BLOCK + HEAD_DIM), 14 * count * width),
        name="local_attention",
    )(q, k, v)


def attend(core, q, within, earlier, carried, gain, mine):
    count, width = q.shape
    heads = width // HEAD_DIM
    per_half = count // BLOCK // 2

    def block(i, core_ref):
        half = core_ref[0] if mine else 1 - core_ref[0]
        return half * per_half + i

    def kernel(core_ref, q_ref, w_ref, e_ref, c_ref, g_ref, o_ref):
        for h in range(heads):
            cols = slice(h * HEAD_DIM, (h + 1) * HEAD_DIM)
            prior = (c_ref[cols, :] + e_ref[0, h]).astype(BF16)
            raw = w_ref[:, cols] + dot(q_ref[:, cols], prior)
            power = jnp.mean(raw * raw, axis=-1, keepdims=True)
            o_ref[:, cols] = (raw * lax.rsqrt(power + 1e-06) * g_ref[:, cols]).astype(BF16)

    return pl.pallas_call(
        kernel,
        grid_spec=pltpu.PrefetchScalarGridSpec(
            num_scalar_prefetch=1,
            grid=(per_half,),
            in_specs=[
                pl.BlockSpec((BLOCK, width), lambda i, c: (block(i, c), 0)),
                pl.BlockSpec((BLOCK, width), lambda i, c: (block(i, c), 0)),
                pl.BlockSpec((1, heads, HEAD_DIM, HEAD_DIM), lambda i, c: (block(i, c), 0, 0, 0)),
                pl.BlockSpec((width, HEAD_DIM), lambda i, c: (0, 0)),
                pl.BlockSpec((1, width), lambda i, c: (0, 0)),
            ],
            out_specs=pl.BlockSpec((BLOCK, width), lambda i, c: (i, 0)),
        ),
        out_shape=jax.ShapeDtypeStruct((count // 2, width), BF16),
        compiler_params=params(),
        cost_estimate=cost(count * width * HEAD_DIM, 4 * count * width),
        name="attend_mine" if mine else "attend_other",
    )(core, q, within, earlier, carried, gain)


def out_project(columns, mine, theirs, w_mine, w_theirs, pieces, added=()):
    rows, depth = mine.shape
    size = rows // 2
    width = depth
    ks = sorted({k for _, k in pieces})
    n_k, n_p = len(ks), len(pieces)

    def kernel(*refs):
        x_ref, y_ref = refs[1:3]
        ws = refs[3 : 3 + 2 * n_k]
        adds = refs[3 + 2 * n_k : 3 + 2 * n_k + len(added)]
        outs = refs[3 + 2 * n_k + len(added) :]
        for p, (r, k) in enumerate(pieces):
            at = slice(r * size, (r + 1) * size)
            j = ks.index(k)
            total = dot(x_ref[at, :], ws[2 * j][...]) + dot(y_ref[at, :], ws[2 * j + 1][...])
            if added:
                total = total + adds[p][...].astype(F32)
            outs[p][...] = total.astype(BF16)

    whole = pl.BlockSpec((rows, depth), lambda i, c: (0, 0))
    piece = pl.BlockSpec((size, width), lambda i, c: (0, 0))
    w_specs = []
    for k in ks:
        w_specs += [pl.BlockSpec((depth, width), lambda i, c, k=k: (0, c[k]))] * 2
    return pl.pallas_call(
        kernel,
        grid_spec=pltpu.PrefetchScalarGridSpec(
            num_scalar_prefetch=1,
            grid=(1,),
            in_specs=[whole, whole] + w_specs + [piece] * len(added),
            out_specs=[piece] * n_p,
        ),
        out_shape=[jax.ShapeDtypeStruct((size, width), BF16)] * n_p,
        compiler_params=params(),
        cost_estimate=cost(4 * size * depth * width * n_p, 4 * depth * width * n_k),
        name="out_" + "_".join(f"{r}{k}" for r, k in pieces),
    )(columns, mine, theirs, *([w_mine, w_theirs] * n_k), *added)


def final_sum(core, groups, count):
    size, width = groups[0][0][0].shape
    terms = len(groups[0][0])
    flat = [t for half in groups for block in half for t in block]

    def kernel(*refs):
        core_ref, ins, o_ref = refs[0], refs[1:-1], refs[-1]
        n = 0
        for which in range(2):
            half = core_ref[0] if which == 0 else 1 - core_ref[0]
            for b in range(2):
                total = ins[n][...].astype(F32)
                for t in range(1, terms):
                    total = total + ins[n + t][...].astype(F32)
                n += terms
                start = pl.multiple_of(half * (2 * size) + b * size, size)
                o_ref[pl.ds(start, size), :] = total.astype(BF16)

    return pl.pallas_call(
        kernel,
        grid_spec=pltpu.PrefetchScalarGridSpec(
            num_scalar_prefetch=1,
            grid=(1,),
            in_specs=[pl.BlockSpec((size, width), lambda i, c: (0, 0))] * len(flat),
            out_specs=pl.BlockSpec((count, width), lambda i, c: (0, 0)),
        ),
        out_shape=jax.ShapeDtypeStruct((count, width), BF16),
        compiler_params=params(),
        cost_estimate=cost(len(flat) * size * width, 2 * len(flat) * size * width),
        name="final_sum",
    )(core, *flat)


RING = 4


def head_send(x, step, cross=0):
    n = 2 * RING
    pairs = [(h, ((h // 2 + step) % RING) * 2 + ((h % 2) ^ cross)) for h in range(n)]
    return lax.ppermute(x, "head", pairs)


def seq_send(x, dz, dx):
    pairs = [
        (s, ((s // RING + dz) % RING) * RING + (s % RING + dx) % RING) for s in range(RING * RING)
    ]
    return lax.ppermute(x, "seq", pairs)


def earlier_shards(total):
    index = lax.axis_index("seq")
    x, z = index % RING, index // RING

    def gather(value, at, send):
        got = [send(value, 1), send(value, -1), send(value, 2)]
        came = [(at + 3) % RING, (at + 1) % RING, (at + 2) % RING]
        got = [g.astype(F32) for g in got]
        before = sum(jnp.where(s < at, g, 0.0) for s, g in zip(came, got))
        return before, got

    before_x, row = gather(total, x, lambda v, d: seq_send(v, 0, d))
    row_total = (total.astype(F32) + row[0] + row[1] + row[2]).astype(BF16)
    before_z, _ = gather(row_total, z, lambda v, d: seq_send(v, d, 0))
    return before_x + before_z


def local(tokens, w_query, w_key, w_value, norm_gain, w_out):
    count = tokens.shape[0]
    place = lax.axis_index("head")
    y, c = place // 2, place % 2
    core = c.astype(jnp.int32).reshape(1)
    chips = jnp.stack([(y + 2) % RING, (y + 1) % RING, (y + 3) % RING, y])
    columns = (chips[:, None] * 2 + jnp.stack([c, 1 - c])[None, :]).reshape(-1).astype(jnp.int32)

    w_theirs = head_send(w_out, 0, 1)
    keys, values, total = project(tokens, [w_key, w_value], True)
    carried = earlier_shards(total)
    (queries,) = project(tokens, [w_query], False)
    within, earlier = local_attention(queries, keys, values)
    gain = norm_gain.reshape(1, -1)
    other = attend(core, queries, within, earlier, carried, gain, False)
    theirs = head_send(other, 0, 1)
    mine = attend(core, queries, within, earlier, carried, gain, True)

    def project_out(pieces, added=()):
        return out_project(columns, mine, theirs, w_out, w_theirs, pieces, added)

    a_s, a_x, b_s, b_x = project_out([(0, 0), (0, 1), (1, 0), (1, 1)])
    a_s, a_x = head_send(a_s, -1), head_send(a_x, -1)
    b_s, b_x = head_send(b_s, 1), head_send(b_x, 1)
    up_s, up_x, down_s, down_x = project_out([(0, 2), (0, 3), (1, 4), (1, 5)])
    first_up = head_send(up_s, 1), head_send(up_x, 1, 1)
    first_down = head_send(down_s, -1), head_send(down_x, -1, 1)
    own = project_out([(0, 6), (1, 6), (0, 7), (1, 7)])
    own_x = head_send(own[2], 0, 1), head_send(own[3], 0, 1)
    up_s, up_x, down_s, down_x = project_out(
        [(1, 2), (1, 3), (0, 4), (0, 5)], (b_s, b_x, a_s, a_x)
    )
    last_up = head_send(up_s, 1), head_send(up_x, 1, 1)
    last_down = head_send(down_s, -1), head_send(down_x, -1, 1)
    groups = [
        [[own[0], first_up[0], last_down[0]], [own[1], first_down[0], last_up[0]]],
        [[own_x[0], first_up[1], last_down[1]], [own_x[1], first_down[1], last_up[1]]],
    ]
    return final_sum(core, groups, count)


def solution(mesh):
    in_specs = (
        P("seq", None),
        P(None, "head"),
        P(None, "head"),
        P(None, "head"),
        P("head"),
        P("head", None),
    )
    out_specs = P("seq", "head")
    return jax.shard_map(local, mesh=mesh, in_specs=in_specs, out_specs=out_specs, check_vma=False)
```

```python
import jax
import jax.numpy as jnp
from jax import lax
from jax.experimental import pallas as pl
from jax.experimental.pallas import tpu as pltpu
from jax.sharding import PartitionSpec as P


HEAD_DIM = 128
BLOCK = 256
RING = 4
F32, BF16 = jnp.float32, jnp.bfloat16
IN_VMEM = pl.BlockSpec(memory_space=pltpu.VMEM)
IN_HBM = pl.BlockSpec(memory_space=pltpu.HBM)
IN_SMEM = pl.BlockSpec(memory_space=pltpu.SMEM)


def dot(a, b):
    return jnp.dot(a, b, preferred_element_type=F32)


def dot_t(a, b, da, db):
    return lax.dot_general(a, b, (((da,), (db,)), ((), ())), preferred_element_type=F32)


def call(kernel, in_specs, out_shape, args, flops, nbytes, mib, scratch=(), aliases=None):
    return pl.pallas_call(
        kernel,
        in_specs=in_specs,
        out_specs=jax.tree.map(lambda _: IN_VMEM, out_shape),
        out_shape=out_shape,
        scratch_shapes=scratch,
        compiler_params=pltpu.CompilerParams(vmem_limit_bytes=mib * 2**20),
        cost_estimate=pl.CostEstimate(
            flops=int(flops), bytes_accessed=int(nbytes), transcendentals=0
        ),
        input_output_aliases=aliases or {},
    )(*args)


def held(x):
    return pltpu.with_memory_space_constraint(x, pltpu.VMEM)


def streamed(x):
    return pltpu.with_memory_space_constraint(x, pltpu.HBM)


SLOTS = 3


def project(tokens, weights, rows, states=False, after=(), into=None, bring=()):
    count, depth = tokens.shape
    width = weights[0].shape[1]
    first, size_m = rows.start, rows.stop - rows.start
    n_w = len(weights)
    big = depth // 4
    sizes = [big // 2, big // 2] + [big] * 3
    starts = [sum(sizes[:k]) for k in range(len(sizes))]
    steps = len(sizes)
    extra = len(after) + (into is not None)

    def kernel(*refs):
        t_hbm, w_hbm = refs[0], refs[1 : 1 + n_w]
        b_hbm = refs[1 + n_w : 1 + n_w + len(bring)]
        rest = refs[1 + n_w + len(bring) + extra :]
        outs, rest = rest[:n_w], rest[n_w:]
        if states:
            s_ref, rest = rest[0], rest[1:]
        if bring:
            b_ref, rest = rest[0], rest[1:]
        t_buf, w_buf, acc, t_sem, w_sem = rest[:5]

        def copies(k):
            at, size, slot = pl.ds(starts[k], sizes[k]), pl.ds(0, sizes[k]), k % SLOTS
            moves = [
                pltpu.make_async_copy(
                    t_hbm.at[pl.ds(first, size_m), at], t_buf.at[slot, :, size], t_sem.at[k]
                )
            ]
            for i in range(n_w):
                moves.append(
                    pltpu.make_async_copy(
                        w_hbm[i].at[at, :], w_buf.at[slot, i, size, :], w_sem.at[k, i]
                    )
                )
            return moves

        brought = [
            pltpu.make_async_copy(
                source, b_ref.at[pl.ds(i * source.shape[0], source.shape[0]), :], rest[5].at[i]
            )
            for i, source in enumerate(b_hbm)
        ]
        for k in range(SLOTS - 1):
            for move in copies(k):
                move.start()
        for k in range(steps):
            for move in copies(k):
                move.wait()
            if k + SLOTS - 1 < steps:
                for move in copies(k + SLOTS - 1):
                    move.start()
            if k + SLOTS == steps:
                for move in brought:
                    move.start()
            slot, size = k % SLOTS, sizes[k]
            for i in range(n_w):
                product = dot(t_buf[slot, :, :size], w_buf[slot, i, :size, :])
                if k == 0:
                    acc[i] = product
                elif k < steps - 1:
                    acc[i] += product
                else:
                    outs[i][first : first + size_m, :] = (acc[i] + product).astype(BF16)
        if states:
            for h in range(width // HEAD_DIM):
                cols = slice(h * HEAD_DIM, (h + 1) * HEAD_DIM)
                s_ref[cols, :] = dot_t(outs[0][:, cols], outs[1][:, cols], 0, 0).astype(BF16)
        for move in brought:
            move.wait()

    out_shape = [pltpu.VMEM((count, width), BF16)] * n_w
    scratch = [
        pltpu.VMEM((SLOTS, size_m, big), BF16),
        pltpu.VMEM((SLOTS, n_w, big, width), BF16),
        pltpu.VMEM((n_w, size_m, width), F32),
        pltpu.SemaphoreType.DMA((steps,)),
        pltpu.SemaphoreType.DMA((steps, n_w)),
    ]
    if states:
        out_shape = out_shape + [pltpu.VMEM((width, HEAD_DIM), BF16)]
    if bring:
        tall = sum(b.shape[0] for b in bring)
        out_shape = out_shape + [pltpu.VMEM((tall, bring[0].shape[1]), BF16)]
        scratch = scratch + [pltpu.SemaphoreType.DMA((len(bring),))]
    in_specs = [IN_HBM] * (1 + n_w + len(bring)) + [pl.BlockSpec(memory_space=pl.ANY)] * len(after)
    args = (streamed(tokens), *map(streamed, weights), *map(streamed, bring), *after)
    aliases = None
    if into is not None:
        aliases = {len(args): 0}
        in_specs, args = in_specs + [IN_VMEM], (*args, into)
    return call(
        kernel,
        in_specs,
        out_shape,
        args,
        2 * size_m * depth * width * n_w,
        2 * depth * (size_m + width * n_w),
        28,
        scratch,
        aliases,
    )


def row_total(total, came, after):
    def kernel(*refs):
        refs[-1][...] = sum((r[...].astype(F32) for r in refs[1:-2]), refs[0][...].astype(F32)).astype(
            BF16
        )

    return call(
        kernel,
        [IN_VMEM] * (1 + len(came)) + [pl.BlockSpec(memory_space=pl.ANY)],
        pltpu.VMEM(total.shape, BF16),
        (total, *came, after),
        4 * total.size,
        8 * total.size,
        4,
    )


def local_attention(q, k, v):
    count, width = q.shape
    heads = width // HEAD_DIM
    blocks = count // BLOCK

    def kernel(q_ref, k_ref, v_ref, w_ref, e_ref):
        rows = lax.broadcasted_iota(jnp.int32, (BLOCK, BLOCK), 0)
        cols = lax.broadcasted_iota(jnp.int32, (BLOCK, BLOCK), 1)
        keep = rows >= cols
        for h in range(heads):
            at_h = slice(h * HEAD_DIM, (h + 1) * HEAD_DIM)
            state = jnp.zeros((HEAD_DIM, HEAD_DIM), F32)
            for b in range(blocks):
                at = slice(b * BLOCK, (b + 1) * BLOCK)
                kb, vb = k_ref[at, at_h], v_ref[at, at_h]
                scores = jnp.where(keep, dot_t(q_ref[at, at_h], kb, 1, 1), 0.0).astype(BF16)
                w_ref[at, at_h] = dot(scores, vb)
                e_ref[b, at_h, :] = state
                if b < blocks - 1:
                    state = state + dot_t(kb, vb, 0, 0)

    return call(
        kernel,
        [IN_VMEM] * 3,
        [pltpu.VMEM((count, width), F32), pltpu.VMEM((blocks, width, HEAD_DIM), F32)],
        (q, k, v),
        4 * count * width * (BLOCK + HEAD_DIM),
        14 * count * width,
        8,
    )


def attend(place, index, q, within, earlier, from_x, from_z, gain, mine, block, after=()):
    count, width = q.shape
    heads = width // HEAD_DIM
    per_half = count // BLOCK // 2
    hops = len(SHIFTS)

    def kernel(place_ref, index_ref, q_ref, w_ref, e_ref, *refs):
        xs, zs, g_ref, o_ref = refs[:hops], refs[hops : 2 * hops], refs[2 * hops], refs[-1]
        half = place_ref[0] % 2 if mine else 1 - place_ref[0] % 2
        at_x, at_z = index_ref[0] % RING, index_ref[0] // RING
        here = half * per_half + block
        rows = pl.ds(pl.multiple_of(here * BLOCK, BLOCK), BLOCK)
        for h in range(heads):
            cols = slice(h * HEAD_DIM, (h + 1) * HEAD_DIM)
            state = e_ref[here, cols, :]
            for at, came in ((at_x, xs), (at_z, zs)):
                for shift, ref in zip(SHIFTS, came):
                    source = (at - shift + RING) % RING
                    state += jnp.where(source < at, ref[cols, :].astype(F32), 0.0)
            raw = w_ref[rows, cols] + dot(q_ref[rows, cols], state.astype(BF16))
            power = jnp.mean(raw * raw, axis=-1, keepdims=True)
            o_ref[:, cols] = (raw * lax.rsqrt(power + 1e-06) * g_ref[:, cols]).astype(BF16)

    return call(
        kernel,
        [IN_SMEM] * 2
        + [IN_VMEM] * (4 + 2 * hops)
        + [pl.BlockSpec(memory_space=pl.ANY)] * len(after),
        pltpu.VMEM((BLOCK, width), BF16),
        (place, index, q, within, earlier, *from_x, *from_z, gain, *after),
        count * width * HEAD_DIM // 2,
        2 * count * width,
        8,
    )


def out_project(place, mine, theirs, w_out, pieces, form, added=(), after=()):
    size, width = mine[0].shape
    n_p = len(pieces)

    def kernel(place_ref, *refs):
        xs, ys, w_ref = refs[:2], refs[2:4], refs[4]
        adds, outs = refs[5 : 5 + len(added)], refs[5 + len(added) + len(after) :]
        y, c = place_ref[0] // 2, place_ref[0] % 2
        for p, (block, step) in enumerate(pieces):
            chip = (y + step + RING) % RING
            for side in range(2):
                core = c if side == 0 else 1 - c
                cols = pl.ds(pl.multiple_of((chip * 2 + core) * width, width), width)
                total = dot(xs[block][...], w_ref[:width, cols])
                total = total + dot(ys[block][...], w_ref[width:, cols])
                here = slice(side * width, (side + 1) * width)
                if added:
                    total = total + adds[p][:, here].astype(F32)
                total = total.astype(BF16)
                if form == "joined":
                    outs[p][:, here] = total
                elif form == "apart":
                    outs[2 * p + side][...] = total
                else:
                    outs[side][p * size : (p + 1) * size, :] = total

    if form == "joined":
        out_shape = [pltpu.VMEM((size, 2 * width), BF16)] * n_p
    elif form == "apart":
        out_shape = [pltpu.VMEM((size, width), BF16)] * (2 * n_p)
    else:
        out_shape = [pltpu.VMEM((n_p * size, width), BF16)] * 2
    return call(
        kernel,
        [IN_SMEM]
        + [IN_VMEM] * (5 + len(added))
        + [pl.BlockSpec(memory_space=pl.ANY)] * len(after),
        out_shape,
        (place, *mine, *theirs, w_out, *added, *after),
        8 * n_p * size * width * width,
        8 * width * width,
        12,
    )


def final_sum(place, own, own_cross, near, late, count):
    size, width = near[0][0].shape

    def kernel(place_ref, own_ref, cross_ref, *refs):
        o_ref = refs[-1]
        c = place_ref[0] % 2
        for which, base in enumerate((own_ref, cross_ref)):
            half = c if which == 0 else 1 - c
            for b in range(2):
                at = slice(b * size, (b + 1) * size)
                total = base[at, :].astype(F32)
                total = total + refs[2 * b + which][...].astype(F32)
                total = total + refs[4 + 2 * b + which][...].astype(F32)
                start = pl.multiple_of(half * (2 * size) + b * size, size)
                o_ref[pl.ds(start, size), :] = total.astype(BF16)

    terms = [a for pair in near for a in pair] + [a for pair in late for a in pair]
    return call(
        kernel,
        [IN_SMEM] + [IN_VMEM] * (2 + len(terms)),
        jax.ShapeDtypeStruct((count, width), BF16),
        (place, own, own_cross, *terms),
        12 * size * width,
        24 * size * width,
        8,
    )


SHIFTS = (1, -1, 2)


def head_send(x, step, cross=0):
    pairs = [
        (h, ((h // 2 + step) % RING) * 2 + ((h % 2) ^ cross)) for h in range(2 * RING)
    ]
    return held(lax.ppermute(x, "head", pairs))


def seq_send(x, dz, dx):
    pairs = [
        (s, ((s // RING + dz) % RING) * RING + (s % RING + dx) % RING) for s in range(RING * RING)
    ]
    return held(lax.ppermute(x, "seq", pairs))


def local(tokens, w_query, w_key, w_value, norm_gain, w_out):
    count = tokens.shape[0]
    place = lax.axis_index("head").astype(jnp.int32).reshape(1)
    index = lax.axis_index("seq").astype(jnp.int32).reshape(1)

    w_theirs = lax.ppermute(w_out, "head", [(h, h ^ 1) for h in range(2 * RING)])
    keys, values, total = project(tokens, [w_key, w_value], slice(0, count), states=True)
    from_x = [seq_send(total, 0, d) for d in SHIFTS]
    cut = count - BLOCK
    queries, w_held = project(
        tokens, [w_query], slice(0, cut), after=(total,), bring=(w_out, w_theirs)
    )
    row = row_total(total, from_x, queries)
    from_z = [seq_send(row, d, 0) for d in SHIFTS]
    (queries,) = project(tokens, [w_query], slice(cut, count), after=(row,), into=queries)
    within, earlier = local_attention(queries, keys, values)

    def attended(mine, block, **kw):
        gain = norm_gain.reshape(1, -1)
        return attend(
            place, index, queries, within, earlier, from_x, from_z, gain, mine, block, **kw
        )

    def project_out(pieces, form, blocks=(0, 1), **kw):
        x, y = [mine[b] for b in blocks], [theirs[b] for b in blocks]
        return out_project(place, x, y, w_held, pieces, form, **kw)

    other0 = attended(False, 0)
    other1 = attended(False, 1, after=(other0,))
    theirs = [head_send(other0, 0, 1), head_send(other1, 0, 1)]
    mine = [attended(True, 0, after=(other1,))]
    (far0,) = project_out([(0, 2)], "joined", blocks=(0, 0))
    mine.append(attended(True, 1, after=(far0,)))
    (far1,) = project_out([(0, 2)], "joined", blocks=(1, 1))
    near = project_out([(0, 1), (1, -1)], "apart", after=(far1,))
    far0, far1 = head_send(far0, -1), head_send(far1, 1)

    def last_hop(up_s, up_x, down_s, down_x):
        up, down = head_send(up_s, 1), head_send(down_s, -1)
        up_x = head_send(up_x, 1, 1)
        return (up, up_x), (down, head_send(down_x, -1, 1))

    own, own_cross = project_out([(0, 0), (1, 0)], "stacked", after=(near[0],))
    near = last_hop(*near)
    own_cross = head_send(own_cross, 0, 1)
    late = project_out([(1, 1), (0, -1)], "apart", added=(far1, far0))
    late = last_hop(*late)[::-1]
    return final_sum(place, own, own_cross, near, late, count)


def solution(mesh):
    in_specs = (
        P("seq", None),
        P(None, "head"),
        P(None, "head"),
        P(None, "head"),
        P("head"),
        P("head", None),
    )
    out_specs = P("seq", "head")
    return jax.shard_map(local, mesh=mesh, in_specs=in_specs, out_specs=out_specs, check_vma=False)
```

```python
import jax
import jax.numpy as jnp
from jax import lax
from jax.experimental import pallas as pl
from jax.experimental.pallas import tpu as pltpu
from jax.sharding import PartitionSpec as P


HEAD_DIM = 128
BLOCK = 256
RING = 4
F32, BF16 = jnp.float32, jnp.bfloat16
IN_VMEM = pl.BlockSpec(memory_space=pltpu.VMEM)
IN_HBM = pl.BlockSpec(memory_space=pltpu.HBM)
IN_SMEM = pl.BlockSpec(memory_space=pltpu.SMEM)


def dot(a, b):
    return jnp.dot(a, b, preferred_element_type=F32)


def dot_t(a, b, da, db):
    return lax.dot_general(a, b, (((da,), (db,)), ((), ())), preferred_element_type=F32)


def call(kernel, in_specs, out_shape, args, flops, nbytes, mib, scratch=(), aliases=None):
    return pl.pallas_call(
        kernel,
        in_specs=in_specs,
        out_specs=jax.tree.map(lambda _: IN_VMEM, out_shape),
        out_shape=out_shape,
        scratch_shapes=scratch,
        compiler_params=pltpu.CompilerParams(vmem_limit_bytes=mib * 2**20),
        cost_estimate=pl.CostEstimate(
            flops=int(flops), bytes_accessed=int(nbytes), transcendentals=0
        ),
        input_output_aliases=aliases or {},
    )(*args)


def held(x):
    return pltpu.with_memory_space_constraint(x, pltpu.VMEM)


def streamed(x):
    return pltpu.with_memory_space_constraint(x, pltpu.HBM)


SLOTS = 3


def project(tokens, weights, rows, states=False, after=(), into=None, bring=()):
    count, depth = tokens.shape
    width = weights[0].shape[1]
    first, size_m = rows.start, rows.stop - rows.start
    n_w = len(weights)
    big = depth // 4
    sizes = [big // 2, big // 2] + [big] * 3
    starts = [sum(sizes[:k]) for k in range(len(sizes))]
    steps = len(sizes)
    extra = len(after) + (into is not None)

    def kernel(*refs):
        t_hbm, w_hbm = refs[0], refs[1 : 1 + n_w]
        b_hbm = refs[1 + n_w : 1 + n_w + len(bring)]
        rest = refs[1 + n_w + len(bring) + extra :]
        outs, rest = rest[:n_w], rest[n_w:]
        if states:
            s_ref, rest = rest[0], rest[1:]
        if bring:
            b_ref, rest = rest[0], rest[1:]
        t_buf, w_buf, acc, t_sem, w_sem = rest[:5]

        def copies(k):
            at, size, slot = pl.ds(starts[k], sizes[k]), pl.ds(0, sizes[k]), k % SLOTS
            moves = [
                pltpu.make_async_copy(
                    t_hbm.at[pl.ds(first, size_m), at], t_buf.at[slot, :, size], t_sem.at[k]
                )
            ]
            for i in range(n_w):
                moves.append(
                    pltpu.make_async_copy(
                        w_hbm[i].at[at, :], w_buf.at[slot, i, size, :], w_sem.at[k, i]
                    )
                )
            return moves

        brought = [
            pltpu.make_async_copy(
                source, b_ref.at[pl.ds(i * source.shape[0], source.shape[0]), :], rest[5].at[i]
            )
            for i, source in enumerate(b_hbm)
        ]
        for k in range(SLOTS - 1):
            for move in copies(k):
                move.start()
        for k in range(steps):
            for move in copies(k):
                move.wait()
            if k + SLOTS - 1 < steps:
                for move in copies(k + SLOTS - 1):
                    move.start()
            if k + SLOTS == steps:
                for move in brought:
                    move.start()
            slot, size = k % SLOTS, sizes[k]
            for i in range(n_w):
                product = dot(t_buf[slot, :, :size], w_buf[slot, i, :size, :])
                if k == 0:
                    acc[i] = product
                elif k < steps - 1:
                    acc[i] += product
                else:
                    outs[i][first : first + size_m, :] = (acc[i] + product).astype(BF16)
        if states:
            for h in range(width // HEAD_DIM):
                cols = slice(h * HEAD_DIM, (h + 1) * HEAD_DIM)
                s_ref[cols, :] = dot_t(outs[0][:, cols], outs[1][:, cols], 0, 0).astype(BF16)
        for move in brought:
            move.wait()

    out_shape = [pltpu.VMEM((count, width), BF16)] * n_w
    scratch = [
        pltpu.VMEM((SLOTS, size_m, big), BF16),
        pltpu.VMEM((SLOTS, n_w, big, width), BF16),
        pltpu.VMEM((n_w, size_m, width), F32),
        pltpu.SemaphoreType.DMA((steps,)),
        pltpu.SemaphoreType.DMA((steps, n_w)),
    ]
    if states:
        out_shape = out_shape + [pltpu.VMEM((width, HEAD_DIM), BF16)]
    if bring:
        tall = sum(b.shape[0] for b in bring)
        out_shape = out_shape + [pltpu.VMEM((tall, bring[0].shape[1]), BF16)]
        scratch = scratch + [pltpu.SemaphoreType.DMA((len(bring),))]
    in_specs = [IN_HBM] * (1 + n_w + len(bring)) + [pl.BlockSpec(memory_space=pl.ANY)] * len(after)
    args = (streamed(tokens), *map(streamed, weights), *map(streamed, bring), *after)
    aliases = None
    if into is not None:
        aliases = {len(args): 0}
        in_specs, args = in_specs + [IN_VMEM], (*args, into)
    return call(
        kernel,
        in_specs,
        out_shape,
        args,
        2 * size_m * depth * width * n_w,
        2 * depth * (size_m + width * n_w),
        28,
        scratch,
        aliases,
    )


def row_total(total, came, after):
    def kernel(*refs):
        refs[-1][...] = sum((r[...].astype(F32) for r in refs[1:-2]), refs[0][...].astype(F32)).astype(
            BF16
        )

    return call(
        kernel,
        [IN_VMEM] * (1 + len(came)) + [pl.BlockSpec(memory_space=pl.ANY)],
        pltpu.VMEM(total.shape, BF16),
        (total, *came, after),
        4 * total.size,
        8 * total.size,
        4,
    )


def local_attention(q, k, v, bring, after):
    count, width = q.shape
    heads = width // HEAD_DIM
    blocks = count // BLOCK

    deep, wide = bring[0].shape
    n_b = len(bring)

    def kernel(q_ref, k_ref, v_ref, *refs):
        b_hbm, (w_ref, e_ref, b_ref, sem) = refs[:n_b], refs[n_b + 1 :]
        moves = [
            pltpu.make_async_copy(source, b_ref.at[pl.ds(i * deep, deep), :], sem.at[i])
            for i, source in enumerate(b_hbm)
        ]
        for move in moves:
            move.start()
        rows = lax.broadcasted_iota(jnp.int32, (BLOCK, BLOCK), 0)
        cols = lax.broadcasted_iota(jnp.int32, (BLOCK, BLOCK), 1)
        keep = rows >= cols
        for h in range(heads):
            at_h = slice(h * HEAD_DIM, (h + 1) * HEAD_DIM)
            state = jnp.zeros((HEAD_DIM, HEAD_DIM), F32)
            for b in range(blocks):
                at = slice(b * BLOCK, (b + 1) * BLOCK)
                kb, vb = k_ref[at, at_h], v_ref[at, at_h]
                scores = jnp.where(keep, dot_t(q_ref[at, at_h], kb, 1, 1), 0.0).astype(BF16)
                w_ref[at, at_h] = dot(scores, vb)
                e_ref[b, at_h, :] = state
                if b < blocks - 1:
                    state = state + dot_t(kb, vb, 0, 0)
        for move in moves:
            move.wait()

    return call(
        kernel,
        [IN_VMEM] * 3 + [IN_HBM] * n_b + [pl.BlockSpec(memory_space=pl.ANY)],
        [
            pltpu.VMEM((count, width), F32),
            pltpu.VMEM((blocks, width, HEAD_DIM), F32),
            pltpu.VMEM((n_b * deep, wide), BF16),
        ],
        (q, k, v, *map(streamed, bring), after),
        4 * count * width * (BLOCK + HEAD_DIM),
        14 * count * width + 2 * n_b * deep * wide,
        12,
        [pltpu.SemaphoreType.DMA((n_b,))],
    )


def attend(place, index, q, within, earlier, from_x, from_z, gain, mine):
    count, width = q.shape
    heads = width // HEAD_DIM
    per_half = count // BLOCK // 2
    hops = len(SHIFTS)

    def kernel(place_ref, index_ref, q_ref, w_ref, e_ref, *refs):
        xs, zs, g_ref, o_ref = refs[:hops], refs[hops : 2 * hops], refs[2 * hops], refs[-1]
        half = place_ref[0] % 2 if mine else 1 - place_ref[0] % 2
        at_x, at_z = index_ref[0] % RING, index_ref[0] // RING
        for h in range(heads):
            cols = slice(h * HEAD_DIM, (h + 1) * HEAD_DIM)
            carried = jnp.zeros((HEAD_DIM, HEAD_DIM), F32)
            for at, came in ((at_x, xs), (at_z, zs)):
                for shift, ref in zip(SHIFTS, came):
                    source = (at - shift + RING) % RING
                    carried += jnp.where(source < at, ref[cols, :].astype(F32), 0.0)
            for b in range(per_half):
                here = half * per_half + b
                rows = pl.ds(pl.multiple_of(here * BLOCK, BLOCK), BLOCK)
                prior = (carried + e_ref[here, cols, :]).astype(BF16)
                raw = w_ref[rows, cols] + dot(q_ref[rows, cols], prior)
                power = jnp.mean(raw * raw, axis=-1, keepdims=True)
                o_ref[b * BLOCK : (b + 1) * BLOCK, cols] = (
                    raw * lax.rsqrt(power + 1e-06) * g_ref[:, cols]
                ).astype(BF16)

    return call(
        kernel,
        [IN_SMEM] * 2 + [IN_VMEM] * (4 + 2 * hops),
        pltpu.VMEM((count // 2, width), BF16),
        (place, index, q, within, earlier, *from_x, *from_z, gain),
        count * width * HEAD_DIM,
        4 * count * width,
        8,
    )


STRAIGHT, CROSS = 0, 1


def out_project(place, mine, theirs, w_out, blocks, added=()):
    rows, width = mine.shape

    def kernel(place_ref, x_ref, y_ref, w_ref, *refs):
        adds, outs = refs[: len(added)], refs[len(added) :]
        y, c = place_ref[0] // 2, place_ref[0] % 2
        for p, (step, side) in enumerate(blocks):
            owner = ((y + step + RING) % RING) * 2 + (c if side == STRAIGHT else 1 - c)
            cols = pl.ds(pl.multiple_of(owner * width, width), width)
            total = dot(x_ref[...], w_ref[:width, cols]) + dot(y_ref[...], w_ref[width:, cols])
            if added:
                total = total + adds[p][...].astype(F32)
            outs[p][...] = total.astype(BF16)

    return call(
        kernel,
        [IN_SMEM] + [IN_VMEM] * (3 + len(added)),
        [pltpu.VMEM((rows, width), BF16)] * len(blocks),
        (place, mine, theirs, w_out, *added),
        4 * len(blocks) * rows * width * width,
        4 * len(blocks) * width * width,
        12,
    )


def final_sum(place, own, near, late):
    rows, width = own[0].shape

    def kernel(place_ref, *refs):
        o_ref = refs[-1]
        c = place_ref[0] % 2
        for which in range(2):
            terms = [refs[2 * i + which][...].astype(F32) for i in range(3)]
            start = pl.multiple_of((c if which == 0 else 1 - c) * rows, rows)
            o_ref[pl.ds(start, rows), :] = (terms[0] + terms[1] + terms[2]).astype(BF16)

    return call(
        kernel,
        [IN_SMEM] + [IN_VMEM] * 6,
        jax.ShapeDtypeStruct((2 * rows, width), BF16),
        (place, *own, *near, *late),
        6 * rows * width,
        16 * rows * width,
        8,
    )


SHIFTS = (1, -1, 2)


def head_send(x, step, cross=0):
    pairs = [
        (h, ((h // 2 + step) % RING) * 2 + ((h % 2) ^ cross)) for h in range(2 * RING)
    ]
    return held(lax.ppermute(x, "head", pairs))


def seq_send(x, dz, dx):
    pairs = [
        (s, ((s // RING + dz) % RING) * RING + (s % RING + dx) % RING) for s in range(RING * RING)
    ]
    return held(lax.ppermute(x, "seq", pairs))


def local(tokens, w_query, w_key, w_value, norm_gain, w_out):
    count = tokens.shape[0]
    place = lax.axis_index("head").astype(jnp.int32).reshape(1)
    index = lax.axis_index("seq").astype(jnp.int32).reshape(1)

    w_theirs = lax.ppermute(w_out, "head", [(h, h ^ 1) for h in range(2 * RING)])
    keys, values, total = project(
        tokens, [w_key, w_value], slice(0, count), states=True, after=(place, index)
    )
    from_x = [seq_send(total, 0, d) for d in SHIFTS]
    (queries,) = project(tokens, [w_query], slice(0, count), after=(total,))
    row = row_total(total, from_x, queries)
    from_z = [seq_send(row, d, 0) for d in SHIFTS]
    within, earlier, w_held = local_attention(
        queries, keys, values, (w_out, w_theirs), row
    )

    def attended(mine):
        gain = norm_gain.reshape(1, -1)
        return attend(place, index, queries, within, earlier, from_x, from_z, gain, mine)

    theirs = head_send(attended(False), 0, 1)
    mine = attended(True)

    def project_out(blocks, **kw):
        return out_project(place, mine, theirs, w_held, blocks, **kw)

    far_s, far_x = project_out([(2, STRAIGHT), (2, CROSS)])
    far_s, far_x = head_send(far_s, -1), head_send(far_x, 1)
    near_s, near_x = project_out([(1, STRAIGHT), (-1, CROSS)])
    near = head_send(near_s, 1), head_send(near_x, -1, 1)
    own_s, own_x = project_out([(0, STRAIGHT), (0, CROSS)])
    own = own_s, head_send(own_x, 0, 1)
    late_s, late_x = project_out([(-1, STRAIGHT), (1, CROSS)], added=(far_s, far_x))
    late = head_send(late_s, -1), head_send(late_x, 1, 1)
    return final_sum(place, own, near, late)


def solution(mesh):
    in_specs = (
        P("seq", None),
        P(None, "head"),
        P(None, "head"),
        P(None, "head"),
        P("head"),
        P("head", None),
    )
    out_specs = P("seq", "head")
    return jax.shard_map(local, mesh=mesh, in_specs=in_specs, out_specs=out_specs, check_vma=False)
```

```python
import jax
import jax.numpy as jnp
from jax import lax
from jax.experimental import pallas as pl
from jax.experimental.pallas import tpu as pltpu
from jax.sharding import PartitionSpec as P


HEAD_DIM = 128
BLOCK = 256
RING = 4
SETS = 2
F32, BF16 = jnp.float32, jnp.bfloat16
IN_VMEM = pl.BlockSpec(memory_space=pltpu.VMEM)
IN_HBM = pl.BlockSpec(memory_space=pltpu.HBM)
IN_SMEM = pl.BlockSpec(memory_space=pltpu.SMEM)


def dot(a, b):
    return jnp.dot(a, b, preferred_element_type=F32)


def dot_t(a, b, da, db):
    return lax.dot_general(a, b, (((da,), (db,)), ((), ())), preferred_element_type=F32)


def call(kernel, in_specs, out_shape, args, flops, nbytes, mib, scratch=(), aliases=None):
    return pl.pallas_call(
        kernel,
        in_specs=in_specs,
        out_specs=jax.tree.map(lambda _: IN_VMEM, out_shape),
        out_shape=out_shape,
        scratch_shapes=scratch,
        compiler_params=pltpu.CompilerParams(vmem_limit_bytes=mib * 2**20),
        cost_estimate=pl.CostEstimate(
            flops=int(flops), bytes_accessed=int(nbytes), transcendentals=0
        ),
        input_output_aliases=aliases or {},
    )(*args)


def held(x):
    return pltpu.with_memory_space_constraint(x, pltpu.VMEM)


def streamed(x):
    return pltpu.with_memory_space_constraint(x, pltpu.HBM)


SLOTS = 3


def project(tokens, weights, ranges, states=False, after=()):
    depth = tokens.shape[1]
    width = weights[0].shape[1]
    count = sum(size for _, size in ranges)
    places = [sum(size for _, size in ranges[:r]) for r in range(len(ranges))]
    n_w, n_r = len(weights), len(ranges)
    big = depth // 4
    sizes = [big // 2, big // 2] + [big] * 3
    starts = [sum(sizes[:k]) for k in range(len(sizes))]
    steps = len(sizes)

    def kernel(*refs):
        t_hbm, w_hbm = refs[0], refs[1 : 1 + n_w]
        rest = refs[1 + n_w + len(after) :]
        outs, rest = rest[:n_w], rest[n_w:]
        if states:
            s_ref, rest = rest[0], rest[1:]
        t_buf, w_buf, acc, t_sem, w_sem = rest

        def copies(k):
            at, size, slot = pl.ds(starts[k], sizes[k]), pl.ds(0, sizes[k]), k % SLOTS
            moves = []
            for r, (first, tall) in enumerate(ranges):
                moves.append(
                    pltpu.make_async_copy(
                        t_hbm.at[pl.ds(first, tall), at],
                        t_buf.at[slot, pl.ds(places[r], tall), size],
                        t_sem.at[k, r],
                    )
                )
            for i in range(n_w):
                moves.append(
                    pltpu.make_async_copy(
                        w_hbm[i].at[at, :], w_buf.at[slot, i, size, :], w_sem.at[k, i]
                    )
                )
            return moves

        for k in range(SLOTS - 1):
            for move in copies(k):
                move.start()
        for k in range(steps):
            for move in copies(k):
                move.wait()
            if k + SLOTS - 1 < steps:
                for move in copies(k + SLOTS - 1):
                    move.start()
            slot, size = k % SLOTS, sizes[k]
            for i in range(n_w):
                product = dot(t_buf[slot, :, :size], w_buf[slot, i, :size, :])
                if k == 0:
                    acc[i] = product
                elif k < steps - 1:
                    acc[i] += product
                else:
                    outs[i][...] = (acc[i] + product).astype(BF16)
        if states:
            for h in range(width // HEAD_DIM):
                cols = slice(h * HEAD_DIM, (h + 1) * HEAD_DIM)
                s_ref[cols, :] = dot_t(outs[0][:, cols], outs[1][:, cols], 0, 0).astype(BF16)

    out_shape = [pltpu.VMEM((count, width), BF16)] * n_w
    if states:
        out_shape = out_shape + [pltpu.VMEM((width, HEAD_DIM), BF16)]
    return call(
        kernel,
        [IN_HBM] * (1 + n_w) + [pl.BlockSpec(memory_space=pl.ANY)] * len(after),
        out_shape,
        (streamed(tokens), *map(streamed, weights), *after),
        2 * count * depth * width * n_w,
        2 * depth * (count + width * n_w),
        28,
        [
            pltpu.VMEM((SLOTS, count, big), BF16),
            pltpu.VMEM((SLOTS, n_w, big, width), BF16),
            pltpu.VMEM((n_w, count, width), F32),
            pltpu.SemaphoreType.DMA((steps, n_r)),
            pltpu.SemaphoreType.DMA((steps, n_w)),
        ],
    )


def row_total(total, came, after):
    def kernel(*refs):
        refs[-1][...] = sum((r[...].astype(F32) for r in refs[1:-2]), refs[0][...].astype(F32)).astype(
            BF16
        )

    return call(
        kernel,
        [IN_VMEM] * (1 + len(came)) + [pl.BlockSpec(memory_space=pl.ANY)],
        pltpu.VMEM(total.shape, BF16),
        (total, *came, after),
        4 * total.size,
        8 * total.size,
        4,
    )


def local_attention(part, q, k, v, bring=(), after=()):
    rows_q, width = q.shape
    heads = width // HEAD_DIM
    blocks = k.shape[0] // BLOCK
    mine = set_blocks(part, blocks)
    n_b = len(bring)

    def kernel(q_ref, k_ref, v_ref, *refs):
        b_hbm, rest = refs[:n_b], refs[n_b + len(after) :]
        w_ref = rest[0]
        moves = []
        if bring:
            e_ref, b_ref, sem = rest[1:]
            deep = b_hbm[0].shape[0]
            moves = [
                pltpu.make_async_copy(source, b_ref.at[pl.ds(i * deep, deep), :], sem.at[i])
                for i, source in enumerate(b_hbm)
            ]
        for move in moves:
            move.start()
        rows = lax.broadcasted_iota(jnp.int32, (BLOCK, BLOCK), 0)
        cols = lax.broadcasted_iota(jnp.int32, (BLOCK, BLOCK), 1)
        keep = rows >= cols
        for h in range(heads):
            at_h = slice(h * HEAD_DIM, (h + 1) * HEAD_DIM)
            state = jnp.zeros((HEAD_DIM, HEAD_DIM), F32)
            for b in range(blocks):
                at = slice(b * BLOCK, (b + 1) * BLOCK)
                kb, vb = k_ref[at, at_h], v_ref[at, at_h]
                if b in mine:
                    at_q = slice(mine.index(b) * BLOCK, (mine.index(b) + 1) * BLOCK)
                    scores = jnp.where(keep, dot_t(q_ref[at_q, at_h], kb, 1, 1), 0.0)
                    w_ref[at_q, at_h] = dot(scores.astype(BF16), vb)
                if bring:
                    e_ref[b, at_h, :] = state
                    if b < blocks - 1:
                        state = state + dot_t(kb, vb, 0, 0)
        for move in moves:
            move.wait()

    out_shape = [pltpu.VMEM((rows_q, width), F32)]
    scratch, nbytes = [], 14 * rows_q * width
    if bring:
        deep, wide = bring[0].shape
        out_shape.append(pltpu.VMEM((blocks, width, HEAD_DIM), F32))
        out_shape.append(pltpu.VMEM((n_b * deep, wide), BF16))
        scratch = [pltpu.SemaphoreType.DMA((n_b,))]
        nbytes += 2 * n_b * deep * wide
    return call(
        kernel,
        [IN_VMEM] * 3
        + [IN_HBM] * n_b
        + [pl.BlockSpec(memory_space=pl.ANY)] * len(after),
        out_shape,
        (q, k, v, *map(streamed, bring), *after),
        4 * rows_q * width * (BLOCK + HEAD_DIM),
        nbytes,
        12,
        scratch,
    )


def set_blocks(part, blocks):
    per_half = blocks // 2 // SETS
    return [half * (blocks // 2) + part * per_half + b for half in range(2) for b in range(per_half)]


def attend(part, place, index, q, within, earlier, from_x, from_z, gain, mine):
    count, width = q.shape
    heads = width // HEAD_DIM
    per_half = count // BLOCK // 2
    hops = len(SHIFTS)

    def kernel(place_ref, index_ref, q_ref, w_ref, e_ref, *refs):
        xs, zs, g_ref, o_ref = refs[:hops], refs[hops : 2 * hops], refs[2 * hops], refs[-1]
        half = place_ref[0] % 2 if mine else 1 - place_ref[0] % 2
        at_x, at_z = index_ref[0] % RING, index_ref[0] // RING
        for h in range(heads):
            cols = slice(h * HEAD_DIM, (h + 1) * HEAD_DIM)
            carried = jnp.zeros((HEAD_DIM, HEAD_DIM), F32)
            for at, came in ((at_x, xs), (at_z, zs)):
                for shift, ref in zip(SHIFTS, came):
                    source = (at - shift + RING) % RING
                    carried += jnp.where(source < at, ref[cols, :].astype(F32), 0.0)
            for b in range(per_half):
                here = half * per_half + b
                rows = pl.ds(pl.multiple_of(here * BLOCK, BLOCK), BLOCK)
                block = (half * SETS + part) * per_half + b
                prior = (carried + e_ref[block, cols, :]).astype(BF16)
                raw = w_ref[rows, cols] + dot(q_ref[rows, cols], prior)
                power = jnp.mean(raw * raw, axis=-1, keepdims=True)
                o_ref[b * BLOCK : (b + 1) * BLOCK, cols] = (
                    raw * lax.rsqrt(power + 1e-06) * g_ref[:, cols]
                ).astype(BF16)

    return call(
        kernel,
        [IN_SMEM] * 2 + [IN_VMEM] * (4 + 2 * hops),
        pltpu.VMEM((count // 2, width), BF16),
        (place, index, q, within, earlier, *from_x, *from_z, gain),
        count * width * HEAD_DIM,
        4 * count * width,
        8,
    )


STRAIGHT, CROSS = 0, 1


def out_project(place, mine, theirs, w_out, blocks, added=(), partial=False):
    terms = [x for x in (mine, theirs) if x is not None]
    rows, width = terms[0].shape

    def kernel(place_ref, *refs):
        xs, w_ref, refs = refs[: len(terms)], refs[len(terms)], refs[len(terms) + 1 :]
        adds, outs = refs[: len(added)], refs[len(added) :]
        y, c = place_ref[0] // 2, place_ref[0] % 2
        for p, (step, side) in enumerate(blocks):
            owner = ((y + step + RING) % RING) * 2 + (c if side == STRAIGHT else 1 - c)
            cols = pl.ds(pl.multiple_of(owner * width, width), width)
            total = adds[p][...].astype(F32) if added else 0.0
            if mine is not None:
                total = total + dot(xs[0][...], w_ref[:width, cols])
            if theirs is not None:
                total = total + dot(xs[-1][...], w_ref[width:, cols])
            outs[p][...] = total.astype(outs[p].dtype)

    return call(
        kernel,
        [IN_SMEM] + [IN_VMEM] * (1 + len(terms) + len(added)),
        [pltpu.VMEM((rows, width), F32 if partial else BF16)] * len(blocks),
        (place, *terms, w_out, *added),
        2 * len(terms) * len(blocks) * rows * width * width,
        2 * len(terms) * len(blocks) * width * width,
        12,
    )


def final_sum(place, part, other, terms, count, into=None):
    rows, width = terms[0].shape

    def kernel(place_ref, *refs):
        total = sum(r[...].astype(F32) for r in refs[1 : len(terms)])
        refs[-1][...] = (refs[0][...].astype(F32) + total).astype(BF16)

    def owner(i, place_ref):
        c = place_ref[0] % 2
        return ((1 - c if other else c) * SETS + part, 0)

    specs = [IN_VMEM] * len(terms)
    args, aliases = (place, *terms), {}
    if into is not None:
        aliases = {len(args): 0}
        specs, args = specs + [pl.BlockSpec(memory_space=pl.ANY)], (*args, into)
    return pl.pallas_call(
        kernel,
        grid_spec=pltpu.PrefetchScalarGridSpec(
            num_scalar_prefetch=1,
            grid=(1,),
            in_specs=specs,
            out_specs=pl.BlockSpec((rows, width), owner),
        ),
        out_shape=jax.ShapeDtypeStruct((count, width), BF16),
        input_output_aliases=aliases,
        compiler_params=pltpu.CompilerParams(vmem_limit_bytes=8 * 2**20),
        cost_estimate=pl.CostEstimate(
            flops=3 * rows * width, bytes_accessed=8 * rows * width, transcendentals=0
        ),
    )(*args)


SHIFTS = (1, -1, 2)


def head_send(x, step, cross=0):
    pairs = [
        (h, ((h // 2 + step) % RING) * 2 + ((h % 2) ^ cross)) for h in range(2 * RING)
    ]
    return held(lax.ppermute(x, "head", pairs))


def seq_send(x, dz, dx):
    pairs = [
        (s, ((s // RING + dz) % RING) * RING + (s % RING + dx) % RING) for s in range(RING * RING)
    ]
    return held(lax.ppermute(x, "seq", pairs))


def local(tokens, w_query, w_key, w_value, norm_gain, w_out):
    count = tokens.shape[0]
    place = lax.axis_index("head").astype(jnp.int32).reshape(1)
    index = lax.axis_index("seq").astype(jnp.int32).reshape(1)

    w_theirs = lax.ppermute(w_out, "head", [(h, h ^ 1) for h in range(2 * RING)])
    keys, values, total = project(
        tokens, [w_key, w_value], [(0, count)], states=True, after=(place, index)
    )
    from_x = [seq_send(total, 0, d) for d in SHIFTS]
    half, rows = count // 2, count // 2 // SETS

    def query(part, after):
        ranges = [(h * half + part * rows, rows) for h in range(2)]
        return project(tokens, [w_query], ranges, after=after)[0]

    queries = query(0, (total,))
    row = row_total(total, from_x, queries)
    from_z = [seq_send(row, d, 0) for d in SHIFTS]
    within, earlier, w_held = local_attention(0, queries, keys, values, (w_out, w_theirs), (row,))
    gain = norm_gain.reshape(1, -1)
    out = None
    for part in range(SETS):
        if part:
            queries = query(part, (within,))
            (within,) = local_attention(part, queries, keys, values)

        def attended(mine):
            return attend(part, place, index, queries, within, earlier, from_x, from_z, gain, mine)

        def send(x, step):
            return head_send(x, step)

        def swap(x):
            return head_send(x, 0, 1)

        theirs = swap(attended(False))
        mine = attended(True)

        def project_out(blocks, mine=mine, theirs=theirs, **kw):
            return out_project(place, mine, theirs, w_held, blocks, **kw)

        blocks = [(2, STRAIGHT), (2, CROSS)]
        begun = project_out(blocks, theirs=None, partial=True)
        far_s, far_x = project_out(blocks, mine=None, added=begun)
        far_s, far_x = send(far_s, -1), send(far_x, 1)
        near_s, near_x = project_out([(1, STRAIGHT), (-1, CROSS)])
        near_s, near_x = send(near_s, 1), send(swap(near_x), -1)
        own_s, own_x = project_out([(0, STRAIGHT), (0, CROSS)])
        own_x = swap(own_x)
        late_s, late_x = project_out([(-1, STRAIGHT), (1, CROSS)], added=(far_s, far_x))
        late_s, late_x = send(late_s, -1), send(swap(late_x), 1)
        out = final_sum(place, part, False, (own_s, near_s, late_s), count, into=out)
        out = final_sum(place, part, True, (own_x, near_x, late_x), count, into=out)
    return out


def solution(mesh):
    in_specs = (
        P("seq", None),
        P(None, "head"),
        P(None, "head"),
        P(None, "head"),
        P("head"),
        P("head", None),
    )
    out_specs = P("seq", "head")
    return jax.shard_map(local, mesh=mesh, in_specs=in_specs, out_specs=out_specs, check_vma=False)
```

```python
import jax
import jax.numpy as jnp
from jax import lax
from jax.experimental import pallas as pl
from jax.experimental.pallas import tpu as pltpu
from jax.sharding import PartitionSpec as P


HEAD_DIM = 128
BLOCK = 256
RING = 4
SETS = 1
F32, BF16 = jnp.float32, jnp.bfloat16
IN_VMEM = pl.BlockSpec(memory_space=pltpu.VMEM)
IN_HBM = pl.BlockSpec(memory_space=pltpu.HBM)
IN_SMEM = pl.BlockSpec(memory_space=pltpu.SMEM)


def dot(a, b):
    return jnp.dot(a, b, preferred_element_type=F32)


def dot_t(a, b, da, db):
    return lax.dot_general(a, b, (((da,), (db,)), ((), ())), preferred_element_type=F32)


def call(kernel, in_specs, out_shape, args, flops, nbytes, mib, scratch=(), aliases=None):
    return pl.pallas_call(
        kernel,
        in_specs=in_specs,
        out_specs=jax.tree.map(lambda _: IN_VMEM, out_shape),
        out_shape=out_shape,
        scratch_shapes=scratch,
        compiler_params=pltpu.CompilerParams(vmem_limit_bytes=mib * 2**20),
        cost_estimate=pl.CostEstimate(
            flops=int(flops), bytes_accessed=int(nbytes), transcendentals=0
        ),
        input_output_aliases=aliases or {},
    )(*args)


def held(x):
    return pltpu.with_memory_space_constraint(x, pltpu.VMEM)


def streamed(x):
    return pltpu.with_memory_space_constraint(x, pltpu.HBM)


SLOTS = 3


def project(tokens, weights, ranges, states=False, after=()):
    depth = tokens.shape[1]
    width = weights[0].shape[1]
    count = sum(size for _, size in ranges)
    places = [sum(size for _, size in ranges[:r]) for r in range(len(ranges))]
    n_w, n_r = len(weights), len(ranges)
    big = depth // 4
    sizes = [big // 2, big // 2] + [big] * 3
    starts = [sum(sizes[:k]) for k in range(len(sizes))]
    steps = len(sizes)

    def kernel(*refs):
        t_hbm, w_hbm = refs[0], refs[1 : 1 + n_w]
        rest = refs[1 + n_w + len(after) :]
        outs, rest = rest[:n_w], rest[n_w:]
        if states:
            s_ref, rest = rest[0], rest[1:]
        t_buf, w_buf, acc, t_sem, w_sem = rest

        def copies(k):
            at, size, slot = pl.ds(starts[k], sizes[k]), pl.ds(0, sizes[k]), k % SLOTS
            moves = []
            for r, (first, tall) in enumerate(ranges):
                moves.append(
                    pltpu.make_async_copy(
                        t_hbm.at[pl.ds(first, tall), at],
                        t_buf.at[slot, pl.ds(places[r], tall), size],
                        t_sem.at[k, r],
                    )
                )
            for i in range(n_w):
                moves.append(
                    pltpu.make_async_copy(
                        w_hbm[i].at[at, :], w_buf.at[slot, i, size, :], w_sem.at[k, i]
                    )
                )
            return moves

        for k in range(SLOTS - 1):
            for move in copies(k):
                move.start()
        for k in range(steps):
            for move in copies(k):
                move.wait()
            if k + SLOTS - 1 < steps:
                for move in copies(k + SLOTS - 1):
                    move.start()
            slot, size = k % SLOTS, sizes[k]
            for i in range(n_w):
                product = dot(t_buf[slot, :, :size], w_buf[slot, i, :size, :])
                if k == 0:
                    acc[i] = product
                elif k < steps - 1:
                    acc[i] += product
                else:
                    outs[i][...] = (acc[i] + product).astype(BF16)
        if states:
            for h in range(width // HEAD_DIM):
                cols = slice(h * HEAD_DIM, (h + 1) * HEAD_DIM)
                s_ref[cols, :] = dot_t(outs[0][:, cols], outs[1][:, cols], 0, 0).astype(BF16)

    out_shape = [pltpu.VMEM((count, width), BF16)] * n_w
    if states:
        out_shape = out_shape + [pltpu.VMEM((width, HEAD_DIM), BF16)]
    return call(
        kernel,
        [IN_HBM] * (1 + n_w) + [pl.BlockSpec(memory_space=pl.ANY)] * len(after),
        out_shape,
        (streamed(tokens), *map(streamed, weights), *after),
        2 * count * depth * width * n_w,
        2 * depth * (count + width * n_w),
        28,
        [
            pltpu.VMEM((SLOTS, count, big), BF16),
            pltpu.VMEM((SLOTS, n_w, big, width), BF16),
            pltpu.VMEM((n_w, count, width), F32),
            pltpu.SemaphoreType.DMA((steps, n_r)),
            pltpu.SemaphoreType.DMA((steps, n_w)),
        ],
    )


def row_total(total, came, after):
    def kernel(*refs):
        refs[-1][...] = sum((r[...].astype(F32) for r in refs[1:-2]), refs[0][...].astype(F32)).astype(
            BF16
        )

    return call(
        kernel,
        [IN_VMEM] * (1 + len(came)) + [pl.BlockSpec(memory_space=pl.ANY)],
        pltpu.VMEM(total.shape, BF16),
        (total, *came, after),
        4 * total.size,
        8 * total.size,
        4,
    )


def local_attention(part, q, k, v, bring=(), after=()):
    rows_q, width = q.shape
    heads = width // HEAD_DIM
    blocks = k.shape[0] // BLOCK
    mine = set_blocks(part, blocks)
    n_b = len(bring)

    def kernel(q_ref, k_ref, v_ref, *refs):
        b_hbm, rest = refs[:n_b], refs[n_b + len(after) :]
        w_ref = rest[0]
        moves = []
        if bring:
            e_ref, b_ref, sem = rest[1:]
            deep = b_hbm[0].shape[0]
            moves = [
                pltpu.make_async_copy(source, b_ref.at[pl.ds(i * deep, deep), :], sem.at[i])
                for i, source in enumerate(b_hbm)
            ]
        for move in moves:
            move.start()
        rows = lax.broadcasted_iota(jnp.int32, (BLOCK, BLOCK), 0)
        cols = lax.broadcasted_iota(jnp.int32, (BLOCK, BLOCK), 1)
        keep = rows >= cols
        for h in range(heads):
            at_h = slice(h * HEAD_DIM, (h + 1) * HEAD_DIM)
            state = jnp.zeros((HEAD_DIM, HEAD_DIM), F32)
            for b in range(blocks):
                at = slice(b * BLOCK, (b + 1) * BLOCK)
                kb, vb = k_ref[at, at_h], v_ref[at, at_h]
                if b in mine:
                    at_q = slice(mine.index(b) * BLOCK, (mine.index(b) + 1) * BLOCK)
                    scores = jnp.where(keep, dot_t(q_ref[at_q, at_h], kb, 1, 1), 0.0)
                    w_ref[at_q, at_h] = dot(scores.astype(BF16), vb)
                if bring:
                    e_ref[b, at_h, :] = state
                    if b < blocks - 1:
                        state = state + dot_t(kb, vb, 0, 0)
        for move in moves:
            move.wait()

    out_shape = [pltpu.VMEM((rows_q, width), F32)]
    scratch, nbytes = [], 14 * rows_q * width
    if bring:
        deep, wide = bring[0].shape
        out_shape.append(pltpu.VMEM((blocks, width, HEAD_DIM), F32))
        out_shape.append(pltpu.VMEM((n_b * deep, wide), BF16))
        scratch = [pltpu.SemaphoreType.DMA((n_b,))]
        nbytes += 2 * n_b * deep * wide
    return call(
        kernel,
        [IN_VMEM] * 3
        + [IN_HBM] * n_b
        + [pl.BlockSpec(memory_space=pl.ANY)] * len(after),
        out_shape,
        (q, k, v, *map(streamed, bring), *after),
        4 * rows_q * width * (BLOCK + HEAD_DIM),
        nbytes,
        12,
        scratch,
    )


def set_blocks(part, blocks):
    per_half = blocks // 2 // SETS
    return [half * (blocks // 2) + part * per_half + b for half in range(2) for b in range(per_half)]


def attend(part, place, index, q, within, earlier, from_x, from_z, gain, mine):
    count, width = q.shape
    heads = width // HEAD_DIM
    per_half = count // BLOCK // 2
    hops = len(SHIFTS)

    def kernel(place_ref, index_ref, q_ref, w_ref, e_ref, *refs):
        xs, zs, g_ref, o_ref = refs[:hops], refs[hops : 2 * hops], refs[2 * hops], refs[-1]
        half = place_ref[0] % 2 if mine else 1 - place_ref[0] % 2
        at_x, at_z = index_ref[0] % RING, index_ref[0] // RING
        for h in range(heads):
            cols = slice(h * HEAD_DIM, (h + 1) * HEAD_DIM)
            carried = jnp.zeros((HEAD_DIM, HEAD_DIM), F32)
            for at, came in ((at_x, xs), (at_z, zs)):
                for shift, ref in zip(SHIFTS, came):
                    source = (at - shift + RING) % RING
                    carried += jnp.where(source < at, ref[cols, :].astype(F32), 0.0)
            for b in range(per_half):
                here = half * per_half + b
                rows = pl.ds(pl.multiple_of(here * BLOCK, BLOCK), BLOCK)
                block = (half * SETS + part) * per_half + b
                prior = (carried + e_ref[block, cols, :]).astype(BF16)
                raw = w_ref[rows, cols] + dot(q_ref[rows, cols], prior)
                power = jnp.mean(raw * raw, axis=-1, keepdims=True)
                o_ref[b * BLOCK : (b + 1) * BLOCK, cols] = (
                    raw * lax.rsqrt(power + 1e-06) * g_ref[:, cols]
                ).astype(BF16)

    return call(
        kernel,
        [IN_SMEM] * 2 + [IN_VMEM] * (4 + 2 * hops),
        pltpu.VMEM((count // 2, width), BF16),
        (place, index, q, within, earlier, *from_x, *from_z, gain),
        count * width * HEAD_DIM,
        4 * count * width,
        8,
    )


STRAIGHT, CROSS = 0, 1
OWN, OUTER, INNER, FAR = range(4)


def chip_of(step, y):
    if step == OUTER:
        return RING - 1 - y
    if step == INNER:
        return y + 1 - 2 * (y % 2)
    return y if step == OWN else (y + 2) % RING


def out_project(place, mine, theirs, w_out, blocks, added=(), partial=False):
    terms = [x for x in (mine, theirs) if x is not None]
    rows, width = terms[0].shape

    def kernel(place_ref, *refs):
        xs, w_ref, refs = refs[: len(terms)], refs[len(terms)], refs[len(terms) + 1 :]
        adds, outs = refs[: len(added)], refs[len(added) :]
        y, c = place_ref[0] // 2, place_ref[0] % 2
        for p, (step, side) in enumerate(blocks):
            owner = chip_of(step, y) * 2 + (c if side == STRAIGHT else 1 - c)
            cols = pl.ds(pl.multiple_of(owner * width, width), width)
            total = adds[p][...].astype(F32) if added else 0.0
            if mine is not None:
                total = total + dot(xs[0][...], w_ref[:width, cols])
            if theirs is not None:
                total = total + dot(xs[-1][...], w_ref[width:, cols])
            outs[p][...] = total.astype(outs[p].dtype)

    return call(
        kernel,
        [IN_SMEM] + [IN_VMEM] * (1 + len(terms) + len(added)),
        [pltpu.VMEM((rows, width), F32 if partial else BF16)] * len(blocks),
        (place, *terms, w_out, *added),
        2 * len(terms) * len(blocks) * rows * width * width,
        2 * len(terms) * len(blocks) * width * width,
        12,
    )


def final_sum(place, part, other, terms, count, into=None):
    rows, width = terms[0].shape

    def kernel(place_ref, *refs):
        total = sum(r[...].astype(F32) for r in refs[1 : len(terms)])
        refs[-1][...] = (refs[0][...].astype(F32) + total).astype(BF16)

    def owner(i, place_ref):
        c = place_ref[0] % 2
        return ((1 - c if other else c) * SETS + part, 0)

    specs = [IN_VMEM] * len(terms)
    args, aliases = (place, *terms), {}
    if into is not None:
        aliases = {len(args): 0}
        specs, args = specs + [pl.BlockSpec(memory_space=pl.ANY)], (*args, into)
    return pl.pallas_call(
        kernel,
        grid_spec=pltpu.PrefetchScalarGridSpec(
            num_scalar_prefetch=1,
            grid=(1,),
            in_specs=specs,
            out_specs=pl.BlockSpec((rows, width), owner),
        ),
        out_shape=jax.ShapeDtypeStruct((count, width), BF16),
        input_output_aliases=aliases,
        compiler_params=pltpu.CompilerParams(vmem_limit_bytes=8 * 2**20),
        cost_estimate=pl.CostEstimate(
            flops=3 * rows * width, bytes_accessed=8 * rows * width, transcendentals=0
        ),
    )(*args)


SHIFTS = (1, -1, 2)


def head_send(x, step, cross=0):
    pairs = [
        (h, chip_of(step, h // 2) * 2 + ((h % 2) ^ cross)) for h in range(2 * RING)
    ]
    return held(lax.ppermute(x, "head", pairs))


def seq_send(x, dz, dx):
    pairs = [
        (s, ((s // RING + dz) % RING) * RING + (s % RING + dx) % RING) for s in range(RING * RING)
    ]
    return held(lax.ppermute(x, "seq", pairs))


def local(tokens, w_query, w_key, w_value, norm_gain, w_out):
    count = tokens.shape[0]
    place = lax.axis_index("head").astype(jnp.int32).reshape(1)
    index = lax.axis_index("seq").astype(jnp.int32).reshape(1)

    w_theirs = lax.ppermute(w_out, "head", [(h, h ^ 1) for h in range(2 * RING)])
    keys, values, total = project(
        tokens, [w_key, w_value], [(0, count)], states=True, after=(place, index)
    )
    from_x = [seq_send(total, 0, d) for d in SHIFTS]
    half, rows = count // 2, count // 2 // SETS

    def query(part, after):
        ranges = [(h * half + part * rows, rows) for h in range(2)]
        return project(tokens, [w_query], ranges, after=after)[0]

    queries = query(0, (total,))
    row = row_total(total, from_x, queries)
    from_z = [seq_send(row, d, 0) for d in SHIFTS]
    within, earlier, w_held = local_attention(0, queries, keys, values, (w_out, w_theirs), (row,))
    gain = norm_gain.reshape(1, -1)
    out = None
    for part in range(SETS):
        if part:
            queries = query(part, (within,))
            (within,) = local_attention(part, queries, keys, values)

        def attended(mine):
            return attend(part, place, index, queries, within, earlier, from_x, from_z, gain, mine)

        def send(x, step):
            return head_send(x, step)

        def swap(x):
            return head_send(x, OWN, 1)

        theirs = swap(attended(False))
        mine = attended(True)

        def project_out(blocks, mine=mine, theirs=theirs, **kw):
            return out_project(place, mine, theirs, w_held, blocks, **kw)

        blocks = [(FAR, STRAIGHT), (FAR, CROSS)]
        begun = project_out(blocks, theirs=None, partial=True)
        far_s, far_x = project_out(blocks, mine=None, added=begun)
        far_s, far_x = send(far_s, OUTER), send(far_x, INNER)
        near_s, near_x = project_out([(OUTER, STRAIGHT), (INNER, CROSS)])
        near_s = send(near_s, OUTER)
        near_x = send(swap(near_x), INNER)
        own_s, own_x = project_out([(OWN, STRAIGHT), (OWN, CROSS)])
        own_x = swap(own_x)
        late_s, late_x = project_out([(INNER, STRAIGHT), (OUTER, CROSS)], added=(far_s, far_x))
        late_s = send(late_s, INNER)
        late_x = send(swap(late_x), OUTER)
        out = final_sum(place, part, True, (own_x, near_x, late_x), count, into=out)
        out = final_sum(place, part, False, (own_s, near_s, late_s), count, into=out)
    return out


def solution(mesh):
    in_specs = (
        P("seq", None),
        P(None, "head"),
        P(None, "head"),
        P(None, "head"),
        P("head"),
        P("head", None),
    )
    out_specs = P("seq", "head")
    return jax.shard_map(local, mesh=mesh, in_specs=in_specs, out_specs=out_specs, check_vma=False)
```
